32 devices in a mesh: groups: 2 (over x), row: 4 (over y, core), col: 4 (over z).
Axes of the slice: x: 2, y: 2, z: 4, core: 2. Of those that a mesh axis runs over, the one named last changes fastest.
Arguments:
- observed: float32 [2048, 2048], P(('groups', 'row'), 'col'), parts along dimension 0, may hold values from -24 to 24
- estimate: float32 [2048, 2048], P(('groups', 'row'), 'col'), parts along dimension 0, may hold values from -6 to 6
- kernel: float32 [512, 256], P(('groups', 'row')), parts along dimension 0, may hold values from -6 to 6
Outputs:
- refined: float32 [2048, 2048], P(('groups', 'row'), 'col'), parts along dimension 0
- new_kernel: float32 [512, 256], P(('groups', 'row')), parts along dimension 0
The draws below stay inside these ranges and needn't reach their ends.
There are 2 independent parts, one for each index of `groups`. The reference program is written for one: setup_inputs(seed, part) draws one part's arguments, and reference() takes and returns one part's arrays. A program takes and returns all parts, laid end to end along the dimension named above; each array names one. Nothing has to cross between parts.
All inputs are finite; a program needn't handle non-finite values.
Results may differ from the reference program's by a relative error of at most 0.0001.
Values sent between devices are 32-bit elements; how exact they have to be, the bound alone decides.
A program may use at most 128 MiB of HBM per device.

```python
import jax
import jax.numpy as jnp

K = 256
ITERS = 1
NR = 1024
NC = 2048


def draw_observed(key, part):
    rows_frac = jnp.arange(NR, dtype=jnp.float32)[:, None] / (NR - 1)
    cols_frac = jnp.arange(NC, dtype=jnp.float32)[None, :] / (NC - 1)
    ramped = 10.0 ** (0.5 * rows_frac + 0.5 * cols_frac)
    values = jnp.clip(jax.random.normal(key, (NR, NC), jnp.float32), -6.0, 6.0)
    return (values * ramped * 0.4).astype(jnp.float32)


def block_scale(stream_key, shape, cuts, low, top_value):
    gain = 1.0
    for axis_at, blocks in cuts:
        steps = jax.random.uniform(jax.random.fold_in(jax.random.fold_in(stream_key, 6), axis_at), (blocks,), jnp.float32, low / len(cuts), top_value / len(cuts))
        gain = gain * jnp.repeat(jnp.exp(steps), shape[axis_at] // blocks).reshape((-1,) + (1,) * (len(shape) - 1 - axis_at))
    return gain


def gaussian(own_key, extent, deviation, reach, pieces=(), held_as=jnp.bfloat16):
    gain = block_scale(own_key, extent, pieces, -0.22, 0.18) if pieces else 1.0
    entries = jax.random.normal(own_key, extent, jnp.float32) * deviation * gain
    return jnp.minimum(jnp.maximum(entries, -reach), reach).astype(held_as)


def setup_inputs(seed: int = 0, part: int = 0) -> dict:
    splits = jax.random.split(jax.random.key(seed), 4)
    part_keys = jax.random.split(jax.random.fold_in(splits[3], part), 4)
    return {
        "observed": draw_observed(jax.random.fold_in(jax.random.fold_in(splits[3], part), 71), part),
        "estimate": gaussian(part_keys[1], (NR, NC), 1.0, 6.0, ((0, 4), (1, 4)), jnp.float32),
        "kernel": gaussian(part_keys[2], (K, K), 1.0, 6.0, ((0, 4),), jnp.float32),
    }


EPSILON = 1e-6


def reference(observed, estimate, kernel):
    half = K // 2
    long_rows = NR + K
    long_cols = NC + K
    factor = 1.0 / K

    def spectrum(field):
        return jnp.fft.rfft2(field, s=(long_rows, long_cols))

    def spatial(spec):
        return jnp.fft.irfft2(spec, s=(long_rows, long_cols))

    image = estimate
    psf = kernel
    for sweep in range(ITERS):
        placed = jnp.pad(psf, ((0, long_rows - K), (0, long_cols - K)))
        placed = jnp.roll(placed, (-half, -half), axis=(0, 1))
        transfer = spectrum(placed)
        image_spec = spectrum(image)
        predicted = spatial(image_spec * transfer)[:NR, :NC] * factor
        residual = predicted - observed
        residual_spec = spectrum(residual)
        image_grad = spatial(residual_spec * jnp.conj(transfer))[:NR, :NC] * factor
        lagged = jnp.roll(spatial(residual_spec * jnp.conj(image_spec)), (half, half), axis=(0, 1))
        psf_grad = lagged[:K, :K] * factor
        loss = 0.5 * jnp.sum(residual * residual)
        image_norm = jnp.sum(image_grad * image_grad)
        psf_norm = jnp.sum(psf_grad * psf_grad)
        image = image - (loss / (image_norm + EPSILON)) * image_grad
        psf = psf - (0.25 * loss / (psf_norm + EPSILON)) * psf_grad
    return image.astype(jnp.float32), psf.astype(jnp.float32)
```

```python
import functools
import math

import jax
import jax.numpy as jnp
import numpy as np
from jax import lax
from jax.experimental import pallas as pl
from jax.experimental.pallas import tpu as pltpu
from jax.sharding import PartitionSpec as P

EPSILON = 1e-06
MESH = pl.DeviceIdType.MESH
VMEM = pltpu.VMEM
AROUND = [(a, b) for a in (-1, 0, 1) for b in (-1, 0, 1) if (a, b) != (0, 0)]


def here(row, col, n_row, n_col):
    return (row >= 0) & (row < n_row) & (col >= 0) & (col < n_col)


def greet(row, col, n_row, n_col):
    barrier = pltpu.get_barrier_semaphore()
    count = n_row + n_col - 2
    for s in range(1, n_row):
        pl.semaphore_signal(
            barrier, inc=1, device_id={"row": lax.rem(row + s, n_row)}, device_id_type=MESH
        )
    for s in range(1, n_col):
        pl.semaphore_signal(
            barrier, inc=1, device_id={"col": lax.rem(col + s, n_col)}, device_id_type=MESH
        )
    for dr, dc in AROUND:
        if dc == 0 or dr == 0:
            continue
        there = here(row + dr, col + dc, n_row, n_col)

        @pl.when(there)
        def _():
            pl.semaphore_signal(
                barrier, inc=1, device_id={"row": row + dr, "col": col + dc}, device_id_type=MESH
            )

        count = count + jnp.where(there, 1, 0)
    pl.semaphore_wait(barrier, count)


BF16 = jnp.bfloat16
F32 = jnp.float32


def spans(tile, margin):
    inner = {-1: (0, margin), 0: (0, tile), 1: (tile - margin, margin)}
    outer = {-1: (tile + margin, margin), 0: (0, tile), 1: (tile, margin)}
    return inner, outer


def at(ref, rows, cols):
    return ref.at[pl.ds(*rows), pl.ds(*cols)]


def folded(x):
    rows, cols = x.shape
    if rows % 8:
        x = jnp.concatenate([x, jnp.zeros((8 - rows % 8, cols), F32)], axis=0)
        rows = x.shape[0]
    x = (x * x).reshape(rows // 8, 8, cols).sum(axis=0)
    total = x[:, :128]
    for at_col in range(128, cols, 128):
        total = total + x[:, at_col : at_col + 128]
    return total


def halves(x):
    high = x.astype(BF16)
    return high, (x - high.astype(F32)).astype(BF16)


def dot3(a, b, flip=False):
    dims = (((1,), (1 if flip else 0,)), ((), ()))
    dot = lambda p, q: lax.dot_general(p, q, dims, preferred_element_type=F32)
    return dot(a[0], b[0]) + (dot(a[0], b[1]) + dot(a[1], b[0]))


def body(
    n_row, n_col, observed, estimate, kernel, t_hi, t_lo, f_hi, f_lo, i_hi, i_lo, refined, new_kernel,
    table, fwd_c, fwd_s, inv_c, inv_s, wide, full, xs, ys, spec_i, spec_k, spec_r, grad, kgrad, land,
    rland, cpart, cland, pieces, srow, scol, sums, *sems,
):
    (hs, hr, ks, kr, bs, br, rs, rr, cs, cr, gs, gr, as_, ar, es, er) = sems
    row, col = lax.axis_index("row"), lax.axis_index("col")
    tile_rows, tile_cols = observed.shape
    owner, side = kernel.shape
    margin = side // 2
    cols_long = tile_cols + side
    rows_long = tile_rows + side
    half = cols_long // 2
    scale = 2.0 / (rows_long * cols_long) / side
    in_r, out_r = spans(tile_rows, margin)
    in_c, out_c = spans(tile_cols, margin)

    def copy(src, dst, ssem, rsem, **target):
        return pltpu.make_async_remote_copy(
            src_ref=src, dst_ref=dst, send_sem=ssem, recv_sem=rsem,
            device_id=target, device_id_type=MESH,
        )

    def halo(i):
        dr, dc = AROUND[i]
        return copy(
            at(estimate, in_r[dr], in_c[dc]), at(wide, out_r[-dr], out_c[-dc]),
            hs.at[i], hr.at[i], row=row + dr, col=col + dc,
        )

    def border(i):
        dr, dc = AROUND[i]
        return copy(
            at(grad, out_r[dr], out_c[dc]), at(land, out_r[dr], out_c[dc]),
            bs.at[i], br.at[i], row=row + dr, col=col + dc,
        )

    def target_of(i):
        dr, dc = AROUND[i]
        return here(row + dr, col + dc, n_row, n_col)

    def source_of(i):
        dr, dc = AROUND[i]
        return here(row - dr, col - dc, n_row, n_col)

    def row_peer(s):
        return lax.rem(row + s, n_row)

    def col_peer(s):
        return lax.rem(col + s, n_col)

    def block(r):
        return pl.ds(pl.multiple_of(r * owner, owner), owner)

    greet(row, col, n_row, n_col)
    gathers = [
        copy(kernel, full.at[block(row), :], ks.at[s - 1], kr.at[s - 1], row=row_peer(s))
        for s in range(1, n_row)
    ]
    for one in gathers:
        one.start()
    for i in range(8):

        @pl.when(target_of(i))
        def _():
            halo(i).start()

    for i, (dr, dc) in enumerate(AROUND):

        @pl.when(jnp.logical_not(source_of(i)))
        def _():
            wide[pl.ds(*out_r[-dr]), pl.ds(*out_c[-dc])] = jnp.zeros(
                (out_r[-dr][1], out_c[-dc][1]), F32
            )

    def angles(high, low, a):
        ch, sh = high[0, pl.ds(a, 1), :], high[1, pl.ds(a, 1), :]
        cl, sl = low[0], low[1]
        return ch * cl - sh * sl, sh * cl + ch * sl

    def fill(high, low, put):
        step = low.shape[1]

        def one(a, _):
            put(pl.ds(pl.multiple_of(a * step, step), step), *angles(high, low, a))
            return 0

        lax.fori_loop(0, high.shape[1], one, 0)

    def put_table(rows, c, s):
        for q, v in enumerate((c, -s)):
            for level, part in enumerate(halves(v)):
                table[level, rows, q * half : (q + 1) * half] = part

    def put_pair(c_ref, s_ref):
        def put(rows, c, s):
            for ref, v in ((c_ref, c), (s_ref, s)):
                for level, part in enumerate(halves(v)):
                    ref[level, rows, :] = part

        return put

    fill(t_hi, t_lo, put_table)
    fill(f_hi, f_lo, put_pair(fwd_c, fwd_s))
    fill(i_hi, i_lo, put_pair(inv_c, inv_s))

    def pair(ref, rows, cols=slice(None)):
        return ref[0, rows, cols], ref[1, rows, cols]

    def store(ref, rows, x):
        high, low = halves(x)
        ref[0, rows, :] = high
        ref[1, rows, :] = low

    lag, own_cols = slice(0, side), slice(margin, margin + tile_cols)
    beside = slice(margin + tile_cols, margin + tile_cols + side)
    all_cols = slice(margin, margin + tile_cols + side)
    near, far = slice(0, tile_rows), slice(tile_rows, rows_long)

    def rows_forward(spec, freqs, x):
        p, q = dot3(pair(fwd_c, freqs), x), dot3(pair(fwd_s, freqs), x)
        spec[freqs, :half] = p[:, :half] + q[:, half:]
        spec[freqs, half:] = p[:, half:] - q[:, :half]

    def rows_inverse(freqs, x):
        p, q = dot3(pair(inv_c, slice(None), freqs), x), dot3(pair(inv_s, slice(None), freqs), x)
        return jnp.concatenate([p[:, :half] - q[:, half:], p[:, half:] + q[:, :half]], axis=1)

    def multiply(dst, a, b, conj):
        def one(k, _):
            rows = pl.ds(pl.multiple_of(k * 32, 32), 32)
            ar_, ai_, br_, bi_ = a[rows, :half], a[rows, half:], b[rows, :half], b[rows, half:]
            if conj:
                re, im = ar_ * br_ + ai_ * bi_, ai_ * br_ - ar_ * bi_
            else:
                re, im = ar_ * br_ - ai_ * bi_, ar_ * bi_ + ai_ * br_
            for q, v in enumerate((re, im)):
                for level, part in enumerate(halves(v)):
                    dst[level, rows, q * half : (q + 1) * half] = part
            return 0

        lax.fori_loop(0, rows_long // 32, one, 0)

    grad[near, :] = dot3(halves(estimate[...]), pair(table, own_cols))

    full[block(row), :] = kernel[...]
    for one in gathers:
        one.wait()
    store(ys, near, dot3(halves(full[...]), pair(table, lag)))
    for freqs in (near, far):
        rows_forward(spec_k, freqs, pair(ys, near))

    for i in range(8):

        @pl.when(source_of(i))
        def _():
            halo(i).wait_recv()

    own = grad[near, :] + dot3(halves(wide[near, tile_cols:]), pair(table, beside))
    other = dot3(halves(wide[far, :]), pair(table, all_cols))
    store(xs, near, own + other)
    store(xs, far, own - other)
    rows_forward(spec_i, near, pair(xs, near))
    rows_forward(spec_i, far, pair(xs, far))
    multiply(xs, spec_i, spec_k, False)
    mixed = rows_inverse(slice(None), pair(xs, slice(None)))
    resid = dot3(halves(mixed), pair(table, own_cols), True) * scale - observed[...]
    sums[0] = folded(resid)
    store(ys, near, dot3(halves(resid), pair(table, own_cols)))
    for freqs in (near, far):
        rows_forward(spec_r, freqs, pair(ys, near))

    multiply(xs, spec_r, spec_i, True)
    mixed = rows_inverse(slice(None), pair(xs, slice(None)))
    kgrad[...] = dot3(halves(mixed), pair(table, lag), True) * scale
    parts = [
        copy(kgrad.at[block(row_peer(s)), :], rland.at[s - 1], rs.at[s - 1], rr.at[s - 1], row=row_peer(s))
        for s in range(1, n_row)
    ]
    for one in parts:
        one.start()

    multiply(xs, spec_r, spec_k, True)
    even = rows_inverse(near, pair(xs, near))
    odd = rows_inverse(far, pair(xs, far))
    store(ys, far, even - odd)
    store(ys, near, even + odd)
    grad[far, :] = dot3(pair(ys, far), pair(table, all_cols), True) * scale
    for i in range(8):
        if AROUND[i][0] != 0:

            @pl.when(target_of(i))
            def _():
                border(i).start()

    grad[near, tile_cols:] = dot3(pair(ys, near), pair(table, beside), True) * scale
    for i in range(8):
        if AROUND[i][0] == 0:

            @pl.when(target_of(i))
            def _():
                border(i).start()

    mine = kgrad[block(row), :]
    for s, one in enumerate(parts):
        one.wait()
        mine = mine + rland[s]
    few = owner // n_col
    for c in range(n_col):
        cpart[c] = mine[c * few : (c + 1) * few]
    parts = [
        copy(cpart.at[col_peer(s)], cland.at[s - 1], cs.at[s - 1], cr.at[s - 1], col=col_peer(s))
        for s in range(1, n_col)
    ]
    for one in parts:
        one.start()
    refined[...] = dot3(pair(ys, near), pair(table, own_cols), True) * scale
    piece = cpart[col]
    for s, one in enumerate(parts):
        one.wait()
        piece = piece + cland[s]
    pieces[col] = piece
    gathers = [
        copy(pieces.at[col], pieces.at[col], gs.at[s - 1], gr.at[s - 1], col=col_peer(s))
        for s in range(1, n_col)
    ]
    for one in gathers:
        one.start()
    sums[2] = folded(piece)
    for i, (dr, dc) in enumerate(AROUND):

        @pl.when(source_of(i))
        def _():
            border(i).wait_recv()
            region = (pl.ds(*in_r[-dr]), pl.ds(*in_c[-dc]))
            refined[region] = refined[region] + land[pl.ds(*out_r[dr]), pl.ds(*out_c[dc])]

    sums[1] = folded(refined[...])
    srow[row] = sums[...]
    parts = [
        copy(srow.at[row], srow.at[row], as_.at[s - 1], ar.at[s - 1], row=row_peer(s))
        for s in range(1, n_row)
    ]
    for one in parts:
        one.start()
    for one in parts:
        one.wait()
    added = srow[0]
    for r in range(1, n_row):
        added = added + srow[r]
    scol[col] = added
    parts = [
        copy(scol.at[col], scol.at[col], es.at[s - 1], er.at[s - 1], col=col_peer(s))
        for s in range(1, n_col)
    ]
    for one in parts:
        one.start()
    for one in gathers:
        one.wait()
    for one in parts:
        one.wait()
    added = scol[0]
    for c in range(1, n_col):
        added = added + scol[c]
    loss = 0.5 * jnp.sum(added[0], keepdims=True)
    image_norm = jnp.sum(added[1], keepdims=True)
    kernel_norm = jnp.sum(added[2], keepdims=True)
    refined[...] = estimate[...] - refined[...] * (loss / (image_norm + EPSILON))
    rate = 0.25 * loss / (kernel_norm + EPSILON)
    for c in range(n_col):
        rows = slice(c * few, (c + 1) * few)
        new_kernel[rows, :] = kernel[rows, :] - pieces[c] * rate
    for i in range(8):

        @pl.when(target_of(i))
        def _():
            halo(i).wait_send()
            border(i).wait_send()


def turns(places, freqs, period, step):
    def both(some, others):
        phase = np.mod(np.outer(some, others), period) * (2 * math.pi / period)
        return jnp.asarray(np.stack([np.cos(phase), np.sin(phase)]).astype(np.float32))

    return both(places[::step], freqs), both(places[:step] - places[0], freqs)


def per_device(n_row, n_col, observed, estimate, kernel):
    tile_rows, tile_cols = observed.shape
    owner, side = kernel.shape
    margin = side // 2
    rows_long, cols_long = tile_rows + side, tile_cols + side
    half = cols_long // 2
    places = np.concatenate([np.arange(cols_long) - margin, np.arange(margin) - margin])
    t_hi, t_lo = turns(places, 2 * np.arange(half) + 1, 2 * cols_long, 16)
    freqs = np.concatenate([np.arange(0, rows_long, 2), np.arange(1, rows_long, 2)])
    centred = np.arange(side) - margin
    i_hi, i_lo = turns(centred, freqs, rows_long, 16)
    f_hi, f_lo = turns(freqs, centred, rows_long, 16)
    dma = pltpu.SemaphoreType.DMA
    more_r, more_c = max(n_row - 1, 1), max(n_col - 1, 1)
    few = owner // n_col
    spectrum = VMEM((rows_long, cols_long), F32)
    split = VMEM((2, rows_long, cols_long), BF16)
    return pl.pallas_call(
        functools.partial(body, n_row, n_col),
        out_shape=(
            jax.ShapeDtypeStruct((tile_rows, tile_cols), F32),
            jax.ShapeDtypeStruct((owner, side), F32),
        ),
        in_specs=[pl.BlockSpec(memory_space=VMEM)] * 9,
        out_specs=(pl.BlockSpec(memory_space=VMEM),) * 2,
        scratch_shapes=[
            VMEM((2, len(places), cols_long), BF16),
            VMEM((2, rows_long, side), BF16),
            VMEM((2, rows_long, side), BF16),
            VMEM((2, side, rows_long), BF16),
            VMEM((2, side, rows_long), BF16),
            spectrum,
            VMEM((side, side), F32),
            split,
            split,
            spectrum,
            spectrum,
            spectrum,
            spectrum,
            VMEM((side, side), F32),
            spectrum,
            VMEM((more_r, owner, side), F32),
            VMEM((n_col, few, side), F32),
            VMEM((more_c, few, side), F32),
            VMEM((n_col, few, side), F32),
            VMEM((n_row, 3, 8, 128), F32),
            VMEM((n_col, 3, 8, 128), F32),
            VMEM((3, 8, 128), F32),
            dma((8,)), dma((8,)),
            dma((more_r,)), dma((more_r,)),
            dma((8,)), dma((8,)),
            dma((more_r,)), dma((more_r,)),
            dma((more_c,)), dma((more_c,)),
            dma((more_c,)), dma((more_c,)),
            dma((more_r,)), dma((more_r,)),
            dma((more_c,)), dma((more_c,)),
        ],
        compiler_params=pltpu.CompilerParams(
            collective_id=0, has_side_effects=True, vmem_limit_bytes=56 * 1024 * 1024
        ),
        name="deconvolve",
    )(observed, estimate, kernel, t_hi, t_lo, f_hi, f_lo, i_hi, i_lo)


def solution(mesh):
    placed = (P(("groups", "row"), "col"), P(("groups", "row"), "col"), P(("groups", "row"), None))
    return jax.shard_map(
        functools.partial(per_device, mesh.shape["row"], mesh.shape["col"]),
        mesh=mesh,
        in_specs=placed,
        out_specs=(P(("groups", "row"), "col"), P(("groups", "row"), None)),
        check_vma=False,
    )
```

```python
import functools
import math

import jax
import jax.numpy as jnp
import numpy as np
from jax import lax
from jax.experimental import pallas as pl
from jax.experimental.pallas import tpu as pltpu
from jax.sharding import PartitionSpec as P

EPSILON = 1e-06
MESH = pl.DeviceIdType.MESH
FEW = 16
VMEM = pltpu.VMEM
AROUND = [(a, b) for a in (-1, 0, 1) for b in (-1, 0, 1) if (a, b) != (0, 0)]


def here(row, col, n_row, n_col):
    return (row >= 0) & (row < n_row) & (col >= 0) & (col < n_col)


def others(n_row, n_col):
    return [(s, t) for s in range(n_row) for t in range(n_col) if (s, t) != (0, 0)]


def peer(row, col, s, t, n_row, n_col):
    return {"row": lax.rem(row + s, n_row), "col": lax.rem(col + t, n_col)}


def greet(row, col, n_row, n_col):
    barrier = pltpu.get_barrier_semaphore()
    if n_row * n_col <= FEW:
        for s, t in others(n_row, n_col):
            pl.semaphore_signal(
                barrier, inc=1, device_id=peer(row, col, s, t, n_row, n_col), device_id_type=MESH
            )
        pl.semaphore_wait(barrier, n_row * n_col - 1)
        return
    count = n_row + n_col - 2
    for s in range(1, n_row):
        pl.semaphore_signal(
            barrier, inc=1, device_id={"row": lax.rem(row + s, n_row)}, device_id_type=MESH
        )
    for s in range(1, n_col):
        pl.semaphore_signal(
            barrier, inc=1, device_id={"col": lax.rem(col + s, n_col)}, device_id_type=MESH
        )
    for dr, dc in AROUND:
        if dc == 0 or dr == 0:
            continue
        there = here(row + dr, col + dc, n_row, n_col)

        @pl.when(there)
        def _():
            pl.semaphore_signal(
                barrier, inc=1, device_id={"row": row + dr, "col": col + dc}, device_id_type=MESH
            )

        count = count + jnp.where(there, 1, 0)
    pl.semaphore_wait(barrier, count)


BF16 = jnp.bfloat16
F32 = jnp.float32


def spans(tile, margin):
    inner = {-1: (0, margin), 0: (0, tile), 1: (tile - margin, margin)}
    outer = {-1: (tile + margin, margin), 0: (0, tile), 1: (tile, margin)}
    return inner, outer


def at(ref, rows, cols):
    return ref.at[pl.ds(*rows), pl.ds(*cols)]


def folded(x):
    rows, cols = x.shape
    if rows % 8:
        x = jnp.concatenate([x, jnp.zeros((8 - rows % 8, cols), F32)], axis=0)
        rows = x.shape[0]
    x = (x * x).reshape(rows // 8, 8, cols).sum(axis=0)
    total = x[:, :128]
    for at_col in range(128, cols, 128):
        total = total + x[:, at_col : at_col + 128]
    return total


def line(x):
    return jnp.sum(folded(x), axis=0, keepdims=True)


def halves(x):
    high = x.astype(BF16)
    return high, (x - high.astype(F32)).astype(BF16)


def dot3(a, b, flip=False):
    dims = (((1,), (1 if flip else 0,)), ((), ()))
    dot = lambda p, q: lax.dot_general(p, q, dims, preferred_element_type=F32)
    return dot(a[0], b[0]) + (dot(a[0], b[1]) + dot(a[1], b[0]))


def body(
    n_row, n_col, observed, estimate, kernel, t_hi, t_lo, f_hi, f_lo, i_hi, i_lo, refined, new_kernel,
    table, fwd_c, fwd_s, inv_c, inv_s, wide, full, xs, ys, spec_i, spec_k, spec_r, grad, kgrad, land,
    rland, cpart, cland, pieces, srow, scol, sums, *sems,
):
    (hs, hr, ks, kr, bs, br, rs, rr, cs, cr, gs, gr, as_, ar, es, er) = sems
    row, col = lax.axis_index("row"), lax.axis_index("col")
    tile_rows, tile_cols = observed.shape
    owner, side = kernel.shape
    margin = side // 2
    cols_long = tile_cols + side
    rows_long = tile_rows + side
    half = cols_long // 2
    scale = 2.0 / (rows_long * cols_long) / side
    in_r, out_r = spans(tile_rows, margin)
    in_c, out_c = spans(tile_cols, margin)

    def copy(src, dst, ssem, rsem, **target):
        return pltpu.make_async_remote_copy(
            src_ref=src, dst_ref=dst, send_sem=ssem, recv_sem=rsem,
            device_id=target, device_id_type=MESH,
        )

    def halo(i):
        dr, dc = AROUND[i]
        return copy(
            at(estimate, in_r[dr], in_c[dc]), at(wide, out_r[-dr], out_c[-dc]),
            hs.at[i], hr.at[i], row=row + dr, col=col + dc,
        )

    def border(i):
        dr, dc = AROUND[i]
        return copy(
            at(grad, out_r[dr], out_c[dc]), at(land, out_r[dr], out_c[dc]),
            bs.at[i], br.at[i], row=row + dr, col=col + dc,
        )

    def target_of(i):
        dr, dc = AROUND[i]
        return here(row + dr, col + dc, n_row, n_col)

    def source_of(i):
        dr, dc = AROUND[i]
        return here(row - dr, col - dc, n_row, n_col)

    def row_peer(s):
        return lax.rem(row + s, n_row)

    def col_peer(s):
        return lax.rem(col + s, n_col)

    def block(r):
        return pl.ds(pl.multiple_of(r * owner, owner), owner)

    greet(row, col, n_row, n_col)
    gathers = [
        copy(kernel, full.at[block(row), :], ks.at[s - 1], kr.at[s - 1], row=row_peer(s))
        for s in range(1, n_row)
    ]
    for one in gathers:
        one.start()
    for i in range(8):

        @pl.when(target_of(i))
        def _():
            halo(i).start()

    for i, (dr, dc) in enumerate(AROUND):

        @pl.when(jnp.logical_not(source_of(i)))
        def _():
            wide[pl.ds(*out_r[-dr]), pl.ds(*out_c[-dc])] = jnp.zeros(
                (out_r[-dr][1], out_c[-dc][1]), F32
            )

    def angles(high, low, a):
        ch, sh = high[0, pl.ds(a, 1), :], high[1, pl.ds(a, 1), :]
        cl, sl = low[0], low[1]
        return ch * cl - sh * sl, sh * cl + ch * sl

    def fill(high, low, put):
        step = low.shape[1]

        def one(a, _):
            put(pl.ds(pl.multiple_of(a * step, step), step), *angles(high, low, a))
            return 0

        lax.fori_loop(0, high.shape[1], one, 0)

    def put_table(rows, c, s):
        for q, v in enumerate((c, -s)):
            for level, part in enumerate(halves(v)):
                table[level, rows, q * half : (q + 1) * half] = part

    def put_pair(c_ref, s_ref):
        def put(rows, c, s):
            for ref, v in ((c_ref, c), (s_ref, s)):
                for level, part in enumerate(halves(v)):
                    ref[level, rows, :] = part

        return put

    fill(t_hi, t_lo, put_table)
    fill(f_hi, f_lo, put_pair(fwd_c, fwd_s))
    fill(i_hi, i_lo, put_pair(inv_c, inv_s))

    def pair(ref, rows, cols=slice(None)):
        return ref[0, rows, cols], ref[1, rows, cols]

    def store(ref, rows, x):
        high, low = halves(x)
        ref[0, rows, :] = high
        ref[1, rows, :] = low

    lag, own_cols = slice(0, side), slice(margin, margin + tile_cols)
    beside = slice(margin + tile_cols, margin + tile_cols + side)
    all_cols = slice(margin, margin + tile_cols + side)
    near, far = slice(0, tile_rows), slice(tile_rows, rows_long)

    def rows_forward(spec, freqs, x):
        p, q = dot3(pair(fwd_c, freqs), x), dot3(pair(fwd_s, freqs), x)
        spec[freqs, :half] = p[:, :half] + q[:, half:]
        spec[freqs, half:] = p[:, half:] - q[:, :half]

    def rows_inverse(freqs, x):
        p, q = dot3(pair(inv_c, slice(None), freqs), x), dot3(pair(inv_s, slice(None), freqs), x)
        return jnp.concatenate([p[:, :half] - q[:, half:], p[:, half:] + q[:, :half]], axis=1)

    def multiply(dst, a, b, conj):
        def one(k, _):
            rows = pl.ds(k * 32, 32)
            ar_, ai_, br_, bi_ = a[rows, :half], a[rows, half:], b[rows, :half], b[rows, half:]
            if conj:
                re, im = ar_ * br_ + ai_ * bi_, ai_ * br_ - ar_ * bi_
            else:
                re, im = ar_ * br_ - ai_ * bi_, ar_ * bi_ + ai_ * br_
            for q, v in enumerate((re, im)):
                for level, part in enumerate(halves(v)):
                    dst[level, rows, q * half : (q + 1) * half] = part
            return 0

        for k in range(rows_long // 32):
            one(k, 0)

    grad[near, :] = dot3(halves(estimate[...]), pair(table, own_cols))

    full[block(row), :] = kernel[...]
    for one in gathers:
        one.wait()
    store(ys, near, dot3(halves(full[...]), pair(table, lag)))
    for freqs in (near, far):
        rows_forward(spec_k, freqs, pair(ys, near))

    for i in range(8):

        @pl.when(source_of(i))
        def _():
            halo(i).wait_recv()

    own = grad[near, :] + dot3(halves(wide[near, tile_cols:]), pair(table, beside))
    other = dot3(halves(wide[far, :]), pair(table, all_cols))
    store(xs, near, own + other)
    store(xs, far, own - other)
    rows_forward(spec_i, near, pair(xs, near))
    rows_forward(spec_i, far, pair(xs, far))
    multiply(xs, spec_i, spec_k, False)
    mixed = rows_inverse(slice(None), pair(xs, slice(None)))
    resid = dot3(halves(mixed), pair(table, own_cols), True) * scale - observed[...]
    sums[...] = jnp.zeros_like(sums)
    sums[0:1] = line(resid)
    store(ys, near, dot3(halves(resid), pair(table, own_cols)))
    for freqs in (near, far):
        rows_forward(spec_r, freqs, pair(ys, near))

    multiply(xs, spec_r, spec_i, True)
    mixed = rows_inverse(slice(None), pair(xs, slice(None)))
    kgrad[...] = dot3(halves(mixed), pair(table, lag), True) * scale
    parts = [
        copy(kgrad.at[block(row_peer(s)), :], rland.at[s - 1], rs.at[s - 1], rr.at[s - 1], row=row_peer(s))
        for s in range(1, n_row)
    ]
    for one in parts:
        one.start()

    multiply(xs, spec_r, spec_k, True)
    even = rows_inverse(near, pair(xs, near))
    odd = rows_inverse(far, pair(xs, far))
    store(ys, far, even - odd)
    store(ys, near, even + odd)
    grad[far, :] = dot3(pair(ys, far), pair(table, all_cols), True) * scale
    for i in range(8):
        if AROUND[i][0] != 0:

            @pl.when(target_of(i))
            def _():
                border(i).start()

    grad[near, tile_cols:] = dot3(pair(ys, near), pair(table, beside), True) * scale
    for i in range(8):
        if AROUND[i][0] == 0:

            @pl.when(target_of(i))
            def _():
                border(i).start()

    mine = kgrad[block(row), :]
    for s, one in enumerate(parts):
        one.wait()
        mine = mine + rland[s]
    few = owner // n_col
    for c in range(n_col):
        cpart[c] = mine[c * few : (c + 1) * few]
    parts = [
        copy(cpart.at[col_peer(s)], cland.at[s - 1], cs.at[s - 1], cr.at[s - 1], col=col_peer(s))
        for s in range(1, n_col)
    ]
    for one in parts:
        one.start()
    refined[...] = dot3(pair(ys, near), pair(table, own_cols), True) * scale
    for i, (dr, dc) in enumerate(AROUND):

        @pl.when(source_of(i))
        def _():
            border(i).wait_recv()
            region = (pl.ds(*in_r[-dr]), pl.ds(*in_c[-dc]))
            refined[region] = refined[region] + land[pl.ds(*out_r[dr]), pl.ds(*out_c[dc])]

    sums[1:2] = line(refined[...])
    piece = cpart[col]
    for s, one in enumerate(parts):
        one.wait()
        piece = piece + cland[s]
    pieces[col] = piece
    sums[2:3] = line(piece)

    gathers = [
        copy(pieces.at[col], pieces.at[col], gs.at[s - 1], gr.at[s - 1], col=col_peer(s))
        for s in range(1, n_col)
    ]

    def total_of(buf):
        added = buf[0]
        for k in range(1, buf.shape[0]):
            added = added + buf[k]
        return added

    if n_row * n_col <= FEW:
        me = row * n_col + col
        srow[me] = sums[...]
        parts = [
            copy(srow.at[me], srow.at[me], as_.at[k], ar.at[k], **peer(row, col, s, t, n_row, n_col))
            for k, (s, t) in enumerate(others(n_row, n_col))
        ]
        for one in parts + gathers:
            one.start()
        for one in parts:
            one.wait()
        added = total_of(srow)
    else:
        srow[row] = sums[...]
        parts = [
            copy(srow.at[row], srow.at[row], as_.at[s - 1], ar.at[s - 1], row=row_peer(s))
            for s in range(1, n_row)
        ]
        for one in parts + gathers:
            one.start()
        for one in parts:
            one.wait()
        scol[col] = total_of(srow)
        parts = [
            copy(scol.at[col], scol.at[col], es.at[s - 1], er.at[s - 1], col=col_peer(s))
            for s in range(1, n_col)
        ]
        for one in parts:
            one.start()
        for one in parts:
            one.wait()
        added = total_of(scol)
    for one in gathers:
        one.wait()
    loss = 0.5 * jnp.sum(added[0:1], keepdims=True)
    image_norm = jnp.sum(added[1:2], keepdims=True)
    kernel_norm = jnp.sum(added[2:3], keepdims=True)
    refined[...] = estimate[...] - refined[...] * (loss / (image_norm + EPSILON))
    rate = 0.25 * loss / (kernel_norm + EPSILON)
    for c in range(n_col):
        rows = slice(c * few, (c + 1) * few)
        new_kernel[rows, :] = kernel[rows, :] - pieces[c] * rate
    for i in range(8):

        @pl.when(target_of(i))
        def _():
            halo(i).wait_send()
            border(i).wait_send()


def turns(places, freqs, period, step):
    def both(some, others):
        phase = np.mod(np.outer(some, others), period) * (2 * math.pi / period)
        return jnp.asarray(np.stack([np.cos(phase), np.sin(phase)]).astype(np.float32))

    return both(places[::step], freqs), both(places[:step] - places[0], freqs)


def per_device(n_row, n_col, observed, estimate, kernel):
    tile_rows, tile_cols = observed.shape
    owner, side = kernel.shape
    margin = side // 2
    rows_long, cols_long = tile_rows + side, tile_cols + side
    half = cols_long // 2
    places = np.concatenate([np.arange(cols_long) - margin, np.arange(margin) - margin])
    t_hi, t_lo = turns(places, 2 * np.arange(half) + 1, 2 * cols_long, 16)
    freqs = np.concatenate([np.arange(0, rows_long, 2), np.arange(1, rows_long, 2)])
    centred = np.arange(side) - margin
    i_hi, i_lo = turns(centred, freqs, rows_long, 16)
    f_hi, f_lo = turns(freqs, centred, rows_long, 16)
    dma = pltpu.SemaphoreType.DMA
    more_r, more_c = max(n_row - 1, 1), max(n_col - 1, 1)
    few = owner // n_col
    firsts = n_row * n_col if n_row * n_col <= FEW else n_row
    spectrum = VMEM((rows_long, cols_long), F32)
    split = VMEM((2, rows_long, cols_long), BF16)
    return pl.pallas_call(
        functools.partial(body, n_row, n_col),
        out_shape=(
            jax.ShapeDtypeStruct((tile_rows, tile_cols), F32),
            jax.ShapeDtypeStruct((owner, side), F32),
        ),
        in_specs=[pl.BlockSpec(memory_space=VMEM)] * 9,
        out_specs=(pl.BlockSpec(memory_space=VMEM),) * 2,
        scratch_shapes=[
            VMEM((2, len(places), cols_long), BF16),
            VMEM((2, rows_long, side), BF16),
            VMEM((2, rows_long, side), BF16),
            VMEM((2, side, rows_long), BF16),
            VMEM((2, side, rows_long), BF16),
            spectrum,
            VMEM((side, side), F32),
            split,
            split,
            spectrum,
            spectrum,
            spectrum,
            spectrum,
            VMEM((side, side), F32),
            spectrum,
            VMEM((more_r, owner, side), F32),
            VMEM((n_col, few, side), F32),
            VMEM((more_c, few, side), F32),
            VMEM((n_col, few, side), F32),
            VMEM((firsts, 8, 128), F32),
            VMEM((n_col, 8, 128), F32),
            VMEM((8, 128), F32),
            dma((8,)), dma((8,)),
            dma((more_r,)), dma((more_r,)),
            dma((8,)), dma((8,)),
            dma((more_r,)), dma((more_r,)),
            dma((more_c,)), dma((more_c,)),
            dma((more_c,)), dma((more_c,)),
            dma((firsts,)), dma((firsts,)),
            dma((more_c,)), dma((more_c,)),
        ],
        compiler_params=pltpu.CompilerParams(
            collective_id=0, has_side_effects=True, vmem_limit_bytes=56 * 1024 * 1024
        ),
        name="deconvolve",
    )(observed, estimate, kernel, t_hi, t_lo, f_hi, f_lo, i_hi, i_lo)


def solution(mesh):
    placed = (P(("groups", "row"), "col"), P(("groups", "row"), "col"), P(("groups", "row"), None))
    return jax.shard_map(
        functools.partial(per_device, mesh.shape["row"], mesh.shape["col"]),
        mesh=mesh,
        in_specs=placed,
        out_specs=(P(("groups", "row"), "col"), P(("groups", "row"), None)),
        check_vma=False,
    )
```
